32 devices in a mesh: group: 2 (over y), row: 4 (over z), col: 4 (over x, core).
Axes of the slice: x: 2, y: 2, z: 4, core: 2. Of those that a mesh axis runs over, the one named last changes fastest.
Arguments:
- tokens: bfloat16 [256, 5120], P('row', ('group', 'col')), may hold values from -6 to 6
- cotangent: bfloat16 [256, 12800], P(('group', 'col'), 'row'), may hold values from -0.375 to 0.375
- master: float32 [12800, 5120], P('row', ('group', 'col')), may hold values from -0.078125 to 0.078125
- moment: float32 [12800, 5120], P('row', ('group', 'col')), may hold values from -6 to 6
- second: float32 [12800, 5120], P('row', ('group', 'col')), may hold values from 0.1 to 4
- prompts: bfloat16 [512, 5120], P(('group', 'col')), may hold values from -6 to 6
- up_weight: bfloat16 [12800, 5120], P('row'), may hold values from -0.078125 to 0.078125
- down_weight: bfloat16 [12800, 5120], P('row'), may hold values from -0.0546875 to 0.0546875
Outputs:
- master_new: float32 [12800, 5120], P('row', ('group', 'col'))
- moment_new: float32 [12800, 5120], P('row', ('group', 'col'))
- second_new: float32 [12800, 5120], P('row', ('group', 'col'))
- prefill: float32 [512, 5120], P(('group', 'col'), 'row')
The draws below stay inside these ranges and needn't reach their ends.
All inputs are finite; a program needn't handle non-finite values.
Results may differ from the reference program's by a relative error of at most 0.0041.
Values may be sent and summed in bfloat16 or wider, within the bound.
No kernel may reach another device: no remote copies, remote signals or barrier semaphores. Data moves between devices by JAX's collectives and lax.ppermute only.
A program may use at most 192 MiB of HBM per device.

```python
import math
import jax
import jax.numpy as jnp

D = 5120
FF = 12800
TOK = 256
PROMPTS = 512


def block_scale(stream_key, extent, cuts, least, top_value):
    gain, own = 1.0, jax.random.fold_in(stream_key, 6)
    for position, shards_of in cuts:
        draws = jnp.exp(jax.random.uniform(jax.random.fold_in(own, position), (shards_of,), jnp.float32, least / len(cuts), top_value / len(cuts)))
        gain = gain * jnp.repeat(draws, extent[position] // shards_of).reshape([-1 if axis == position else 1 for axis in range(len(extent))])
    return gain


def gaussian(own_key, shape, deviation, bound, cuts=(), held_as=jnp.bfloat16):
    values = deviation * jax.random.normal(own_key, shape, jnp.float32)
    if cuts:
        values = values * block_scale(own_key, shape, cuts, -0.22, 0.18)
    return jnp.clip(values, -bound, bound).astype(held_as)


def setup_inputs(seed: int = 0) -> dict:
    arg_keys = jax.random.split(jax.random.key(seed), 9)
    return {
        "tokens": gaussian(arg_keys[0], (TOK, D), 1.0, 6.0, ((0, 4), (1, 8))),
        "cotangent": gaussian(arg_keys[1], (TOK, FF), (TOK ** -0.5), 0.375, ((0, 8), (1, 4))),
        "master": gaussian(arg_keys[2], (FF, D), D ** -0.5, 0.078125, ((0, 4), (1, 8)), jnp.float32),
        "moment": gaussian(arg_keys[3], (FF, D), 1.0, 6.0, ((0, 4), (1, 8)), jnp.float32),
        "second": jnp.clip(jnp.exp(math.log(4.0) - 3.6888794 * jax.random.uniform(arg_keys[4], (FF, D), jnp.float32) ** block_scale(arg_keys[4], (FF, D), ((0, 4), (1, 8)), -0.2, 0.2)), 0.1, 4.0),
        "prompts": gaussian(arg_keys[5], (PROMPTS, D), 1.0, 6.0, ((0, 8),)),
        "up_weight": gaussian(arg_keys[6], (FF, D), D ** -0.5, 0.078125, ((0, 4),)),
        "down_weight": gaussian(arg_keys[7], (FF, D), FF ** -0.5, 0.0546875, ((0, 4),)),
    }


beta_first = 0.9
beta_second = 0.95
learn_rate = 0.002
weight_decay = 0.1
epsilon = 1e-08
first_bias = 1.0 - 0.9 ** 10
second_bias = 1.0 - 0.95 ** 10

def adam_update(gradient, master, moment, second):
    moment_new = beta_first * moment + (1.0 - beta_first) * gradient
    second_new = beta_second * second + (1.0 - beta_second) * gradient * gradient
    direction = moment_new / first_bias / (jnp.sqrt(second_new / second_bias) + epsilon)
    master_new = master - learn_rate * (direction + weight_decay * master)
    return (master_new, moment_new, second_new)

def reference(tokens, cotangent, master, moment, second, prompts, up_weight, down_weight):
    gradient = jnp.dot(cotangent.T, tokens, preferred_element_type=jnp.float32)
    master_new, moment_new, second_new = adam_update(gradient, master, moment, second)
    refreshed = master_new.astype(jnp.bfloat16)
    gate_pre = jnp.dot(prompts, refreshed.T, preferred_element_type=jnp.float32)
    up_pre = jnp.dot(prompts, up_weight.T, preferred_element_type=jnp.float32)
    hidden = (jax.nn.silu(gate_pre) * up_pre).astype(jnp.bfloat16)
    prefill = jnp.dot(hidden, down_weight, preferred_element_type=jnp.float32)
    return (master_new, moment_new, second_new, prefill)
```

```python
import functools

import jax
import jax.numpy as jnp
from jax import lax
from jax.experimental import pallas as pl
from jax.experimental.pallas import tpu as pltpu
from jax.sharding import PartitionSpec as P


beta_first = 0.9
beta_second = 0.95
learn_rate = 0.002
weight_decay = 0.1
epsilon = 1e-08
first_bias = 1.0 - 0.9**10
second_bias = 1.0 - 0.95**10


bf16 = jnp.bfloat16
f32 = jnp.float32
lanes = 128
tile_choice = (640, 512, 384, 256, 128)


def adam_update(gradient, master, moment, second):
    moment_new = beta_first * moment + (1.0 - beta_first) * gradient
    second_new = beta_second * second + (1.0 - beta_second) * gradient * gradient
    direction = moment_new / first_bias / (jnp.sqrt(second_new / second_bias) + epsilon)
    master_new = master - learn_rate * (direction + weight_decay * master)
    return (master_new, moment_new, second_new)


def adam_folded(gradient, master, moment, second):
    moment_new = beta_first * moment + (1.0 - beta_first) * gradient
    second_new = beta_second * second + ((1.0 - beta_second) * gradient) * gradient
    scaled = second_new * (1.0 / second_bias)
    root = scaled * lax.rsqrt(scaled) + epsilon
    master_new = (1.0 - learn_rate * weight_decay) * master - (learn_rate / first_bias) * moment_new / root
    return (master_new, moment_new, second_new)


def plain(tokens, cotangent, master, moment, second, prompts, up_weight, down_weight):
    cotangent_all = lax.all_gather(cotangent, ("group", "col"), axis=0, tiled=True)
    gradient = jnp.einsum(
        "tf,td->fd",
        cotangent_all,
        lax.all_gather(tokens, "row", axis=0, tiled=True),
        preferred_element_type=f32,
    )
    master_new, moment_new, second_new = adam_update(gradient, master, moment, second)
    refreshed = master_new.astype(bf16)
    prompt_cols = lax.all_to_all(prompts, ("group", "col"), split_axis=1, concat_axis=0, tiled=True)
    gate_pre = lax.psum_scatter(
        jnp.einsum("nd,fd->nf", prompt_cols, refreshed, preferred_element_type=f32),
        ("group", "col"),
        scatter_dimension=0,
        tiled=True,
    )
    up_pre = jnp.einsum("nd,fd->nf", prompts, up_weight, preferred_element_type=f32)
    hidden = (jax.nn.silu(gate_pre) * up_pre).astype(bf16)
    prefill = lax.psum_scatter(
        jnp.einsum("fd,nf->dn", down_weight, hidden, preferred_element_type=f32),
        "row",
        scatter_dimension=0,
        tiled=True,
    ).T
    return (master_new, moment_new, second_new, prefill)


def full(shape):
    return pl.BlockSpec(shape, lambda *a: (0,) * len(shape))


resident = pl.BlockSpec(memory_space=pltpu.VMEM)


def params(mebibytes):
    return pltpu.CompilerParams(vmem_limit_bytes=mebibytes << 20)


def prompt_tiles(where, own, other, tile, count, at):
    rows = own.shape[0]

    def kernel(where_ref, own_ref, other_ref, *tile_refs):
        core = where_ref[0]
        for j in range(count):
            cols = pl.ds(pl.multiple_of(where_ref[at + j] * tile, lanes), tile)
            for ref, side in ((own_ref, core), (other_ref, 1 - core)):
                to = pl.ds(pl.multiple_of(side * rows, rows), rows)
                tile_refs[j][to, :] = ref[:, cols]

    return pl.pallas_call(
        kernel,
        grid_spec=pltpu.PrefetchScalarGridSpec(
            num_scalar_prefetch=1, grid=(1,), in_specs=[resident] * 2, out_specs=[resident] * count
        ),
        out_shape=[jax.ShapeDtypeStruct((2 * rows, tile), bf16)] * count,
        compiler_params=params(8),
        name="prompt_tiles",
    )(where, own, other)


def up_product(where, own, other, up_weight, tile):
    rows, width = own.shape
    hidden = up_weight.shape[0]
    half = tile // 2

    def kernel(where_ref, own_ref, other_ref, w_ref, o_ref, held):
        @pl.when(pl.program_id(0) == 0)
        def _():
            core = where_ref[0]
            for ref, side in ((own_ref, core), (other_ref, 1 - core)):
                held[pl.ds(pl.multiple_of(side * rows, rows), rows), :] = ref[...]

        o_ref[...] = lax.dot_general(
            w_ref[...], held[...], (((1,), (1,)), ((), ())), preferred_element_type=f32
        )

    return pl.pallas_call(
        kernel,
        grid_spec=pltpu.PrefetchScalarGridSpec(
            num_scalar_prefetch=1,
            grid=(hidden // tile,),
            in_specs=[
                full((rows, width)),
                full((rows, width)),
                pl.BlockSpec((half, width), lambda i, w: (2 * i + w[0], 0)),
            ],
            out_specs=pl.BlockSpec((half, 2 * rows), lambda i, w: (i, 0)),
            scratch_shapes=[pltpu.VMEM((2 * rows, width), bf16)],
        ),
        out_shape=jax.ShapeDtypeStruct((hidden // 2, 2 * rows), f32),
        compiler_params=params(24),
        cost_estimate=pl.CostEstimate(
            flops=2 * hidden * rows * width, transcendentals=0, bytes_accessed=hidden * width
        ),
        name="up_product",
    )(where, own, other, up_weight)


def fetch(arrays):
    n = len(arrays)

    def kernel(*refs):
        copies = [pltpu.make_async_copy(refs[i], refs[n + i], refs[2 * n].at[i]) for i in range(n)]
        for copy in copies:
            copy.start()
        for copy in copies:
            copy.wait()

    return pl.pallas_call(
        kernel,
        in_specs=[pl.BlockSpec(memory_space=pl.ANY)] * n,
        out_specs=[resident] * n,
        out_shape=[jax.ShapeDtypeStruct(a.shape, a.dtype) for a in arrays],
        scratch_shapes=[pltpu.SemaphoreType.DMA((n,))],
        compiler_params=params(8),
        cost_estimate=pl.CostEstimate(
            flops=0, transcendentals=0, bytes_accessed=sum(a.size * a.dtype.itemsize for a in arrays)
        ),
        name="fetch",
    )(*arrays)


def refresh(where, pieces, token_pieces, prompt_cols, state, previous, tile, first, count):
    hidden, width = state[0].shape
    half = tile // 2
    n, q, z = len(pieces), len(prompt_cols), len(token_pieces)
    step = pieces[0].shape[0]
    rows = prompt_cols[0].shape[0]
    spread = token_pieces[0].shape[0]
    orders = 5

    def kernel(where_ref, *refs):
        piece_refs, refs = refs[:n], refs[n:]
        token_refs, refs = refs[:z], refs[z:]
        col_refs, refs = refs[:q], refs[q:]
        state_refs, refs = refs[:3], refs[3:]
        refs = refs[len(previous) :]
        new_refs, refs = refs[:3], refs[3:]
        send_ref, keep_ref, window, turned, held, token_ref = refs
        i, s = pl.program_id(0), pl.program_id(1)
        core = where_ref[0]

        @pl.when((i == 0) & (s == 0))
        def _():
            for j in range(q):
                turned[:, j * rows : (j + 1) * rows] = col_refs[j][...].T
            for m in range(z):
                to = pl.ds(pl.multiple_of(where_ref[orders + m] * spread, spread), spread)
                held[to, :] = token_refs[m][...]
            for j in range(n):
                source = pl.ds(pl.multiple_of(where_ref[orders + z + j] * step, step), step)
                token_ref[j * step : (j + 1) * step, :] = held[source, :]

        @pl.when(s == 0)
        def _():
            cols = pl.ds(pl.multiple_of((first + i) * tile, lanes), tile)
            window[...] = jnp.concatenate([ref[:, cols] for ref in piece_refs], axis=0).T

        side = jnp.where(s == 0, 1 - core, core)
        part = jnp.dot(
            window[pl.ds(pl.multiple_of(side * half, half), half), :],
            token_ref[...],
            preferred_element_type=f32,
        )
        at = pl.ds(pl.multiple_of((2 * (first + i) + side) * half, half), half)
        new = adam_folded(part, *[ref[at, :] for ref in state_refs])
        for ref, value in zip(new_refs, new):
            ref[...] = value
        product = jnp.dot(new[0].astype(bf16), turned[...], preferred_element_type=f32)
        to = pl.ds(pl.multiple_of(i * half, half), half)

        @pl.when(s == 0)
        def _():
            send_ref[to, :] = product.astype(send_ref.dtype)

        @pl.when(s == 1)
        def _():
            keep_ref[to, :] = product.astype(keep_ref.dtype)

    def at(i, s, w):
        return (2 * (first + i) + jnp.where(s == 0, 1 - w[0], w[0]), 0)

    block = pl.BlockSpec((half, width), at)
    out = [jax.ShapeDtypeStruct((hidden, width), f32)] * 3
    out += [jax.ShapeDtypeStruct((count * half, q * rows), t) for t in (bf16, f32)]
    return pl.pallas_call(
        kernel,
        grid_spec=pltpu.PrefetchScalarGridSpec(
            num_scalar_prefetch=1,
            grid=(count, 2),
            in_specs=[resident] * (n + z + q + 3) + [pl.BlockSpec(memory_space=pl.ANY)] * len(previous),
            out_specs=[block] * 3 + [resident] * 2,
            scratch_shapes=[
                pltpu.VMEM((tile, n * step), bf16),
                pltpu.VMEM((width, q * rows), bf16),
                pltpu.VMEM((n * step, width), bf16),
                pltpu.VMEM((n * step, width), bf16),
            ],
        ),
        out_shape=out,
        input_output_aliases={1 + n + z + q + 3 + m: m for m in range(len(previous))},
        compiler_params=params(16),
        cost_estimate=pl.CostEstimate(
            flops=2 * count * tile * width * (n * step + q * rows),
            transcendentals=count * tile * width,
            bytes_accessed=24 * count * tile * width,
        ),
        name="refresh",
    )(where, *pieces, *token_pieces, *prompt_cols, *state, *previous)


def join_cores(keep, received, rows):
    parts = []
    for j in range(keep.shape[1] // rows):
        cut = slice(j * rows, (j + 1) * rows)
        total = keep[:, cut] + received[:, cut].astype(f32)
        parts.append(total.astype(bf16) if j else total)
    return parts


def activate(own, received, up_pre):
    for value in received:
        own = own + value.astype(f32)
    return (jax.nn.silu(own) * up_pre).astype(bf16)


def down_product(where, own, other, down_weight, tile, cols, types, slots):
    hidden = down_weight.shape[0]
    half = tile // 2
    n = len(own)
    rows = own[0].shape[1]
    counts = [a.shape[0] // half for a in own]

    def kernel(where_ref, *refs):
        own_refs, other_refs, w_ref = refs[:n], refs[n : 2 * n], refs[2 * n]
        out_refs, (held, turned) = refs[2 * n + 1 : -2], refs[-2:]
        core = where_ref[0]
        i = pl.program_id(0)

        @pl.when(i == 0)
        def _():
            base = 0
            for c in range(n):
                for t in range(counts[c]):
                    for ref, side in ((own_refs[c], core), (other_refs[c], 1 - core)):
                        at = pl.multiple_of(base + side * half, half)
                        held[pl.ds(at, half), :] = ref[t * half : (t + 1) * half, :]
                    base += tile
            turned[...] = held[...].T

        product = jnp.dot(turned[...], w_ref[...], preferred_element_type=f32)
        for j in range(len(types)):

            @pl.when(i == j)
            def _():
                out_refs[j][...] = product.astype(types[j])

    def at(i, w):
        return (0, 2 * w[slots + i] + w[0])

    return pl.pallas_call(
        kernel,
        grid_spec=pltpu.PrefetchScalarGridSpec(
            num_scalar_prefetch=1,
            grid=(len(types),),
            in_specs=[full(a.shape) for a in own + other] + [pl.BlockSpec((hidden, cols), at)],
            out_specs=[full((rows, cols))] * len(types),
            scratch_shapes=[pltpu.VMEM((hidden, rows), bf16), pltpu.VMEM((rows, hidden), bf16)],
        ),
        out_shape=[jax.ShapeDtypeStruct((rows, cols), t) for t in types],
        compiler_params=params(24),
        cost_estimate=pl.CostEstimate(
            flops=2 * hidden * rows * cols * len(types),
            transcendentals=0,
            bytes_accessed=2 * hidden * cols * len(types),
        ),
        name="down_product",
    )(where, *own, *other, down_weight)


def staged(sizes, tile, tokens, cotangent, master, moment, second, prompts, up_weight, down_weight):
    groups, rows, cols = sizes
    chips = cols // 2
    plane = ("group", "col")
    offsets = [(g, x) for g in range(groups) for x in range(chips)]
    offsets = [o for o in offsets if o != (0, 0)]

    def move(value, dg, dx, dk=0):
        pairs = []
        for g in range(groups):
            for c in range(cols):
                x, k = c // 2, c % 2
                to = ((x + dx) % chips) * 2 + (k + dk) % 2
                pairs.append((g * cols + c, ((g + dg) % groups) * cols + to))
        return lax.ppermute(value, plane, pairs)

    def swap(value):
        return move(value, 0, 0, 1)

    def row_swap(value, bit):
        return lax.ppermute(value, "row", [(i, i ^ bit) for i in range(rows)])

    group, row, col = (lax.axis_index(a) for a in ("group", "row", "col"))
    chip, core = col // 2, col % 2

    def place(dg, dx, k):
        return ((group + dg) % groups) * cols + ((chip + dx) % chips) * 2 + k

    relative = [0]
    bit = rows // 2
    while bit:
        relative += [m ^ bit for m in relative]
        bit //= 2
    index = [core, row ^ 3, row ^ 1, row ^ 2, row] + [row ^ m for m in relative]
    for k in (core, 1 - core):
        index += [place(0, 0, k)] + [place(-o[0], -o[1], k) for o in offsets]
    tiles_at = len(index)
    index += [place(0, 0, core)] + [place(*o, core) for o in offsets]
    where = jnp.stack(index)

    other_prompts = swap(prompts)
    tiles = prompt_tiles(
        where, prompts, other_prompts, master.shape[1], 1 + len(offsets), tiles_at
    )
    tiles, cotangent, tokens = lax.optimization_barrier((tiles, cotangent, tokens))
    prompt_cols, own = [tiles[0]], [cotangent]
    for o, tile_of in zip(offsets, tiles[1:]):
        own.append(move(cotangent, *o))
        prompt_cols.append(move(tile_of, *o))

    token_pieces = [tokens]
    bit = rows // 2
    while bit:
        both = jnp.concatenate(token_pieces, 0)
        token_pieces = [both, row_swap(both, bit)]
        bit //= 2
    spread = tokens.shape[0]
    token_pieces = [t[m : m + spread] for t in token_pieces for m in range(0, t.shape[0], spread)]

    state = fetch((master, moment, second))
    pieces = own + [swap(p) for p in own]

    total_tiles = master.shape[0] // tile
    head = (total_tiles + 1) // 2
    new = ()
    gates = []
    for first, count in ((0, head), (head, total_tiles - head)):
        *new, send, keep = refresh(
            where, pieces, token_pieces, prompt_cols, state, new, tile, first, count
        )
        mine, *away = join_cores(keep, swap(send), prompt_cols[0].shape[0])
        mine, away, new = lax.optimization_barrier((mine, away, new))
        back = [move(a, -o[0], -o[1]) for a, o in zip(away, offsets)]
        gates.append((mine, back))
    up_pre = up_product(where, prompts, other_prompts, up_weight, tile)
    acts = []
    at = 0
    for mine, back in gates:
        acts.append(activate(mine, back, up_pre[at : at + mine.shape[0]]))
        at += mine.shape[0]
    others = [swap(a) for a in acts]

    out_cols = down_weight.shape[1] // rows // 2
    far_pair, across = down_product(where, acts, others, down_weight, tile, out_cols, (bf16, bf16), 1)
    far, mine = down_product(where, acts, others, down_weight, tile, out_cols, (f32, f32), 3)
    from_pair = row_swap(far_pair, 1)
    from_near = row_swap(across, 1)
    from_far = row_swap((far + from_pair.astype(f32)).astype(bf16), 2)
    total = mine + from_near.astype(f32) + from_far.astype(f32)
    half = total.shape[0] // 2
    stay = lax.dynamic_slice_in_dim(total, core * half, half, 0)
    leave = swap(lax.dynamic_slice_in_dim(total, (1 - core) * half, half, 0))
    prefill = jnp.where(
        core == 0, jnp.concatenate([stay, leave], 1), jnp.concatenate([leave, stay], 1)
    )
    return (*new, prefill)


def shards(sizes, *arrays):
    tokens, cotangent, master, _, _, prompts, _, down_weight = arrays
    groups, rows, cols = sizes
    hidden, width = master.shape
    tiles = [t for t in tile_choice if hidden % t == 0 and hidden // t > 1 and t % 32 == 0]
    fits = (
        tiles
        and rows == 4
        and cols % 2 == 0
        and groups * cols > 2
        and width % lanes == 0
        and prompts.shape[0] * 2 == lanes
        and cotangent.shape[0] % 16 == 0
        and tokens.shape[0] % 16 == 0
        and down_weight.shape[1] % (2 * rows * lanes) == 0
    )
    if not fits:
        return plain(*arrays)
    return staged(sizes, tiles[0], *arrays)


def solution(mesh):
    in_specs = (
        P("row", ("group", "col")),
        P(("group", "col"), "row"),
        P("row", ("group", "col")),
        P("row", ("group", "col")),
        P("row", ("group", "col")),
        P(("group", "col"), None),
        P("row", None),
        P("row", None),
    )
    out_specs = (
        P("row", ("group", "col")),
        P("row", ("group", "col")),
        P("row", ("group", "col")),
        P(("group", "col"), "row"),
    )
    sizes = tuple(mesh.shape[a] for a in ("group", "row", "col"))
    return jax.shard_map(
        functools.partial(shards, sizes), mesh=mesh, in_specs=in_specs, out_specs=out_specs, check_vma=False
    )
```
